32 devices in a mesh: land: 8 (over y, x, core), sea: 4 (over z).
Axes of the slice: x: 2, y: 2, z: 4, core: 2. Of those that a mesh axis runs over, the one named last changes fastest.
Arguments:
- adj_depth: float32 [4096, 2048], P('land', 'sea'), may hold values from -6 to 6
- conductance: float32 [4096, 2048], P('land', 'sea'), may hold values from 0.02 to 0.24
- wet: int32 [4, 4096, 2048], P(None, 'land', 'sea'), may hold values 0 or 1
- coast_cell: int32 [262144], P(('land', 'sea')), may hold values from 0 to 262143
- coast_dest: int32 [262144, 1], P(('land', 'sea')), may hold values from 0 to 31; in each aligned block of 8192 rows (0 to 8191, 8192 to 16383, ...) at most 512 rows name the same one
- coast_node: int32 [262144], P(('land', 'sea')), may hold values from 0 to 16383
- coast_weight: float32 [262144], P(('land', 'sea')), may hold values from 0.2 to 2
- adj_ocean: float32 [4096, 128], P(('land', 'sea')), may hold values from -6 to 6
- ocean_blocks: bfloat16 [4096, 2, 128, 128], P(('land', 'sea')), may hold values from -0.375 to 0.375
- ocean_target: int32 [4096, 2], P(('land', 'sea')), may hold values from 0 to 511
Outputs:
- land_out: float32 [4096, 2048], P('land', 'sea')
- ocean_out: float32 [4096, 128], P(('land', 'sea'))
The draws below stay inside these ranges and needn't reach their ends.
Inputs may be any that keep to these rules, and one draw needn't show every extreme that they name: `coast_dest`: in each device's 8192 rows no partition is named by more than 512 entries, and one is named by exactly 512. `ocean_target`: blocks are numbered within the group of the 4 devices that share a land index.
All inputs are finite; a program needn't handle non-finite values. No bound on the sum of `wet` on one device may be relied on, other than what follows from the above.
Results may differ from the reference program's by a relative error of at most 0.0036.
Values sent between devices are 32-bit elements; how exact they have to be, the bound alone decides.
A program may use at most 128 MiB of HBM per device.

```python
import math
import jax
import jax.numpy as jnp
import numpy as np
from jax import lax

RX = 512
RY = 512
NB = 128
BS = 128
KB = 2
CL = 8192
STEPS = 4
MOST = 512
NXR = 4096
NYR = 2048
OBLK = 512
NBLK = 4096
NCOAST = 262144
N_SEA = 4
DEVICES = 32


def with_ends(result, stream_key, low, high):
    longest = result.shape.index(max(result.shape))
    spots = []
    for shift in (0, 1):
        where = [jax.random.randint(jax.random.fold_in(stream_key, axis), (), 0, length) for axis, length in enumerate(result.shape)]
        where[longest] = (where[longest] + shift) % result.shape[longest]
        spots.append(tuple(where))
    return result.at[spots[0]].set(low).at[spots[1]].set(high)


def levels(own_key, dims, pieces, low, top_value):
    factor_of, own = 1.0, jax.random.fold_in(own_key, 6)
    for position, shards_of in pieces:
        steps = jnp.exp(jax.random.uniform(jax.random.fold_in(own, position), (shards_of,), jnp.float32, low / len(pieces), top_value / len(pieces)))
        factor_of = factor_of * jnp.repeat(steps, dims[position] // shards_of).reshape([-1 if axis == position else 1 for axis in range(len(dims))])
    return factor_of


def shared_out(rng, own, number, rows, amount, top, limit, lean):
    ranking = jax.random.permutation(rng, amount)
    crowded, common = portions_of(amount, rows * top, limit, lean, True), portions_of(amount, rows * top, limit, lean, False)
    places = jnp.arange(amount)

    def named(tallies, offset_by):
        used = int((tallies > 0).sum())
        fixed = max(1, used // 4)
        shifted = fixed + (places - fixed + offset_by * (used - fixed)) % max(1, amount - fixed)
        return jnp.zeros((amount,), jnp.int32).at[ranking[jnp.where(places < fixed, places, shifted)]].set(jnp.asarray(tallies, jnp.int32))

    tallies = jnp.where(number % 4 == 0, named(crowded, number // 4), named(common, number - number // 4 - 1))
    mixed = jax.random.permutation(jax.random.fold_in(own, 3), amount)
    donor, taker = mixed[0:amount // 2 * 2:2], mixed[1:amount // 2 * 2:2]
    slack = jnp.minimum(tallies[donor] - 1, limit - tallies[taker]) // 2
    slack = jnp.where((donor == ranking[0]) | (taker == ranking[0]) | (tallies[taker] == 0), 0, jnp.maximum(slack, 0))
    shifted = jax.random.randint(jax.random.fold_in(own, 4), (amount // 2,), 0, 1 << 20) % (slack + 1)
    tallies = tallies.at[donor].add(-shifted).at[taker].add(shifted)
    items = jnp.searchsorted(jnp.cumsum(tallies), jnp.arange(rows * top), side="right").astype(jnp.int32)
    table = items.reshape(top, rows).T
    table = table[jax.random.permutation(jax.random.fold_in(own, 1), rows)]
    offset_by = jax.random.randint(jax.random.fold_in(own, 2), (rows, 1), 0, top)
    return jnp.take_along_axis(table, (jnp.arange(top)[None, :] + offset_by) % top, axis=1)


def portions_of(amount, total, limit, skew, full):
    loads = [(1 << 20) // math.isqrt(rank ** skew) + 1 for rank in range(1, amount + 1)]
    largest = limit if full else min(limit, max(-(-total // amount), total * loads[0] // sum(loads)))
    least = 1 if total - largest >= amount - 1 else 0
    given, rest = [largest] + [least] * (amount - 1), total - largest - least * (amount - 1)
    while rest > 0:
        movable = [i for i in range(1, amount) if given[i] < largest] or [i for i in range(1, amount) if given[i] < limit]
        mass, left = sum([loads[i] for i in movable]), rest
        for i in movable:
            more = min(limit - given[i], max(1, left * loads[i] // mass), rest)
            given[i] = given[i] + more
            rest = rest - more
    return np.array(given)


def centred(stream_key, shape, scale, limit, pieces=(), dtype=jnp.bfloat16):
    entries = jax.random.normal(stream_key, shape, jnp.float32) * scale
    if len(pieces) > 0:
        entries = levels(stream_key, shape, pieces, -0.22, 0.18) * entries
    return jnp.clip(entries, min=-limit, max=limit).astype(dtype)


def setup_inputs(seed: int = 0) -> dict:
    key_list = jax.random.split(jax.random.key(seed), 11)
    adj_depth = centred(key_list[0], (NXR, NYR), 1.0, 6.0, ((0, 8), (1, 4)), jnp.float32)
    conductance = jnp.clip(0.02 + 0.22 * jax.random.uniform(key_list[1], (NXR, NYR), jnp.float32) ** levels(key_list[1], (NXR, NYR), ((0, 8), (1, 4)), -0.2, 0.2), 0.02, 0.24)
    wet = with_ends((jax.random.randint(key_list[2], (STEPS, NXR, NYR), 0, 4) < 3).astype(jnp.int32), jax.random.fold_in(key_list[2], 1), 0, 1)
    coast_cell = with_ends(jax.random.randint(key_list[3], (NCOAST,), 0, RX * RY), jax.random.fold_in(key_list[3], 1), 0, (RX * RY) - 1).astype(jnp.int32)
    coast_dest_keys = jax.random.split(jax.random.fold_in(key_list[4], 1), NCOAST // CL)
    coast_dest_turns = jax.random.permutation(jax.random.fold_in(key_list[4], 3), NCOAST // CL)
    coast_dest = jax.vmap(lambda own, number: shared_out(jax.random.fold_in(key_list[4], 2), own, number, CL, DEVICES, 1, MOST, 2))(coast_dest_keys, coast_dest_turns).reshape((NCOAST, 1))
    coast_node = with_ends(jax.random.randint(key_list[5], (NCOAST,), 0, NB * BS), jax.random.fold_in(key_list[5], 1), 0, (NB * BS) - 1).astype(jnp.int32)
    coast_weight = jnp.clip(jnp.exp(math.log(2.0) - 2.3025851 * jax.random.uniform(key_list[6], (NCOAST,), jnp.float32) ** levels(key_list[6], (NCOAST,), ((0, 32),), -0.2, 0.2)), 0.2, 2.0)
    adj_ocean = centred(key_list[7], (NBLK, BS), 1.0, 6.0, ((0, 32),), jnp.float32)
    ocean_blocks = centred(key_list[8], (NBLK, KB, BS, BS), (BS * KB) ** -0.5, 0.375, ((0, 32),))
    ocean_target = with_ends(jax.random.randint(key_list[9], (NBLK, KB), 0, OBLK), jax.random.fold_in(key_list[9], 1), 0, OBLK - 1).astype(jnp.int32)
    return dict(adj_depth=adj_depth, conductance=conductance, wet=wet, coast_cell=coast_cell, coast_dest=coast_dest, coast_node=coast_node, coast_weight=coast_weight, adj_ocean=adj_ocean, ocean_blocks=ocean_blocks, ocean_target=ocean_target)


def laplace_zero(spread):
    padded = jnp.pad(spread, 1)
    beside_all = padded[2:, 1:-1] + padded[:-2, 1:-1] + padded[1:-1, 2:] + padded[1:-1, :-2]
    return beside_all - 4.0 * spread


def block_terms(pair):
    weights, vector = pair
    return jnp.einsum("bkij,bi->bkj", weights.astype(jnp.float32), vector.astype(jnp.float32))


def reference(adj_depth, conductance, wet, coast_cell, coast_dest, coast_node, coast_weight, adj_ocean, ocean_blocks, ocean_target):
    source_dev = (jnp.arange(DEVICES * CL) // CL).astype(jnp.int32)
    cell_row = (source_dev // N_SEA) * RX + coast_cell // RY
    cell_col = (source_dev % N_SEA) * RY + coast_cell % RY
    node_global = coast_dest[:, 0] * (NB * BS) + coast_node
    block_dev = (jnp.arange(DEVICES * NB) // NB).astype(jnp.int32)
    target_global = ((block_dev // N_SEA) * (NB * N_SEA))[:, None] + ocean_target
    target_global = target_global.reshape(-1)
    land_adj = adj_depth
    ocean_adj = adj_ocean
    grouped = ocean_blocks.reshape(DEVICES, NB, KB, BS, BS)
    for timestep in range(STEPS):
        wet_now = wet[timestep].astype(jnp.float32)
        flux = coast_weight * wet_now[cell_row, cell_col] * land_adj[cell_row, cell_col]
        coupled = jnp.zeros((NB * DEVICES * BS,), jnp.float32).at[node_global].add(flux)
        coupled = coupled.reshape(NB * DEVICES, BS)
        ocean_low = ocean_adj.astype(jnp.bfloat16)
        terms = lax.map(block_terms, (grouped, ocean_low.reshape(DEVICES, NB, BS)))
        partial_sum = jnp.zeros((NB * DEVICES, BS), jnp.float32).at[target_global].add(terms.reshape(-1, BS))
        ocean_adj = 0.5 * ocean_adj + partial_sum + coupled
        spread = conductance * wet_now * land_adj
        land_adj = land_adj + laplace_zero(spread)
    return land_adj, ocean_adj
```

```python
import functools

import jax
import jax.numpy as jnp
from jax import lax
from jax.experimental import pallas as pl
from jax.experimental.pallas import tpu as pltpu
from jax.sharding import PartitionSpec as P

STEPS = 4
LANES = 128
SUB = 8
HALO = STEPS


def exchanged(last, first, axis):
    count = lax.axis_size(axis)
    forward = [(i, i + 1) for i in range(count - 1)]
    backward = [(target, source) for source, target in forward]
    return lax.ppermute(last, axis, forward), lax.ppermute(first, axis, backward)


def fields(depth, conductance, wet, rows, columns):
    return jnp.concatenate(
        [
            depth[None, rows, columns],
            conductance[None, rows, columns],
            wet[:, rows, columns].astype(jnp.float32),
        ],
        axis=0,
    )


def land_kernel(depth, cond, wet, left, right, top, bottom, out, masked, ext):
    rows, cols = depth.shape
    mid_r, mid_c = pl.ds(SUB, rows), pl.ds(LANES, cols)
    ext[0, mid_r, mid_c] = depth[...]
    ext[1, mid_r, mid_c] = cond[...]
    for t in range(STEPS):
        ext[2 + t, mid_r, mid_c] = wet[t].astype(jnp.float32)
    for i in range(2 + STEPS):
        ext[i, mid_r, pl.ds(0, LANES)] = left[i]
        ext[i, mid_r, pl.ds(LANES + cols, LANES)] = right[i]
        ext[i, pl.ds(0, SUB), :] = top[i]
        ext[i, pl.ds(SUB + rows, SUB), :] = bottom[i]
    height, width = ext.shape[1], ext.shape[2]
    for t in range(STEPS):
        wet_land = ext[2 + t] * ext[0]
        masked[t] = wet_land[SUB : SUB + rows, LANES : LANES + cols].astype(jnp.bfloat16)
        spread = ext[1] * wet_land
        beside = (
            pltpu.roll(spread, 1, 0)
            + pltpu.roll(spread, height - 1, 0)
            + pltpu.roll(spread, 1, 1)
            + pltpu.roll(spread, width - 1, 1)
        )
        ext[0] = ext[0] + (beside - 4.0 * spread)
    out[...] = ext[0, mid_r, mid_c]


def land_steps(depth, cond, wet):
    rows, cols = depth.shape
    every = slice(None)
    pick = functools.partial(fields, depth, cond, wet)
    first_c = pick(every, slice(0, HALO))
    last_c = pick(every, slice(cols - HALO, cols))
    left, right = exchanged(
        last_c.transpose(0, 2, 1), first_c.transpose(0, 2, 1), "sea"
    )
    left, right = left.transpose(0, 2, 1), right.transpose(0, 2, 1)

    def wide(where):
        return jnp.concatenate(
            [left[:, where], pick(where, every), right[:, where]], axis=2
        )

    top, bottom = exchanged(
        wide(slice(rows - HALO, rows)), wide(slice(0, HALO)), "land"
    )
    side = LANES - HALO
    left = jnp.pad(left, ((0, 0), (0, 0), (side, 0)))
    right = jnp.pad(right, ((0, 0), (0, 0), (0, side)))
    top = jnp.pad(top, ((0, 0), (SUB - HALO, 0), (side, side)))
    bottom = jnp.pad(bottom, ((0, 0), (0, SUB - HALO), (side, side)))
    return pl.pallas_call(
        land_kernel,
        out_shape=(
            jax.ShapeDtypeStruct((rows, cols), jnp.float32),
            jax.ShapeDtypeStruct((STEPS, rows, cols), jnp.bfloat16),
        ),
        scratch_shapes=[
            pltpu.VMEM((2 + STEPS, rows + 2 * SUB, cols + 2 * LANES), jnp.float32)
        ],
        compiler_params=pltpu.CompilerParams(vmem_limit_bytes=48 << 20),
        name="land_steps",
    )(depth, cond, wet, left, right, top, bottom)


def iota(shape, axis):
    return lax.broadcasted_iota(jnp.int32, shape, axis)


def halves(value):
    high = value.astype(jnp.bfloat16).astype(jnp.float32)
    return high, value - high


def across(a, b):
    return lax.dot_general(
        a, b, (((1,), (1,)), ((), ())), preferred_element_type=jnp.float32
    )


def placed(row, lane, values, rows):
    count = row.shape[1]
    row_hot = jnp.where(iota((rows, count), 0) == row, 1.0, 0.0).astype(jnp.bfloat16)
    lane_is = iota((LANES, count), 0) == lane
    spreads = [jnp.where(lane_is, v, 0.0).astype(jnp.bfloat16) for v in values]
    return across(row_hot, jnp.concatenate(spreads, axis=0))


def send_kernel(capacity, piece, cell, dest, node, weight, masked, out, acc, carry):
    step = pl.program_id(0)
    devices = carry.shape[0]
    cols = masked.shape[2]
    count = cell.shape[2]

    @pl.when(step == 0)
    def _():
        acc[...] = jnp.zeros_like(acc)
        carry[...] = jnp.zeros_like(carry)

    dest_now = dest[0]
    matches = jnp.where(iota((devices, count), 0) == dest_now, 1.0, 0.0)
    triangle = jnp.where(
        iota((piece, piece), 0) <= iota((piece, piece), 1), 1.0, 0.0
    ).astype(jnp.bfloat16)
    base = carry[:, 0:1]
    ranks = []
    for p in range(count // piece):
        own = matches[:, p * piece : (p + 1) * piece]
        running = jnp.dot(
            own.astype(jnp.bfloat16), triangle, preferred_element_type=jnp.float32
        )
        ranks.append(jnp.sum(own * (running + base), axis=0, keepdims=True))
        base = base + jnp.sum(own, axis=1, keepdims=True)
    carry[...] = jnp.broadcast_to(base, carry.shape)
    rank = jnp.concatenate(ranks, axis=1).astype(jnp.int32) - 1
    slot = dest_now * capacity + rank

    place = cell[0]
    cell_row, cell_col = place // cols, place % cols
    col_hot = jnp.where(iota((cols, count), 0) == cell_col, 1.0, 0.0).astype(jnp.bfloat16)
    row_is = iota((masked.shape[1], count), 0) == cell_row
    values = []
    for t in range(STEPS):
        lines = jnp.dot(masked[t], col_hot, preferred_element_type=jnp.float32)
        found = jnp.sum(jnp.where(row_is, lines, 0.0), axis=0, keepdims=True)
        values.extend(halves(weight[0] * found))
    node_now = node[0]
    values.append((node_now // LANES).astype(jnp.float32))
    values.append((node_now % LANES).astype(jnp.float32))
    acc[...] += placed(slot // LANES, slot % LANES, values, acc.shape[0])

    @pl.when(step == pl.num_programs(0) - 1)
    def _():
        def block(i):
            return acc[:, i * LANES : (i + 1) * LANES]

        for t in range(STEPS):
            out[t] = block(2 * t) + block(2 * t + 1)
        out[STEPS] = block(2 * STEPS) * float(LANES) + block(2 * STEPS + 1)


def packed(masked, cell, dest, node, weight, devices):
    entries = cell.shape[0]
    count = 1024
    steps = entries // count
    capacity = 2 * entries // devices
    rows = devices * capacity // LANES
    line = pl.BlockSpec((1, 1, count), lambda i: (i, 0, 0))
    shape = (steps, 1, count)
    return pl.pallas_call(
        functools.partial(send_kernel, capacity, 256),
        grid=(steps,),
        in_specs=[line] * 4 + [pl.BlockSpec(masked.shape, lambda i: (0, 0, 0))],
        out_specs=pl.BlockSpec((STEPS + 1, rows, LANES), lambda i: (0, 0, 0)),
        out_shape=jax.ShapeDtypeStruct((STEPS + 1, rows, LANES), jnp.float32),
        scratch_shapes=[
            pltpu.VMEM((rows, (2 * STEPS + 2) * LANES), jnp.float32),
            pltpu.VMEM((devices, LANES), jnp.float32),
        ],
        compiler_params=pltpu.CompilerParams(vmem_limit_bytes=48 << 20),
        name="coast_pack",
    )(cell.reshape(shape), dest.reshape(shape), node.reshape(shape), weight.reshape(shape), masked)


def couple_kernel(got, out, acc):
    step = pl.program_id(0)

    @pl.when(step == 0)
    def _():
        acc[...] = jnp.zeros_like(acc)

    node = got[STEPS : STEPS + 1, :].astype(jnp.int32)
    values = []
    for t in range(STEPS):
        values.extend(halves(got[t : t + 1, :]))
    acc[...] += placed(node // LANES, node % LANES, values, acc.shape[0])

    @pl.when(step == pl.num_programs(0) - 1)
    def _():
        for t in range(STEPS):
            at = 2 * t * LANES
            out[t] = acc[:, at : at + LANES] + acc[:, at + LANES : at + 2 * LANES]


def coupled_steps(got, blocks):
    slots = got.shape[1]
    count = 2048
    return pl.pallas_call(
        couple_kernel,
        grid=(slots // count,),
        in_specs=[pl.BlockSpec((STEPS + 1, count), lambda i: (0, i))],
        out_specs=pl.BlockSpec((STEPS, blocks, LANES), lambda i: (0, 0, 0)),
        out_shape=jax.ShapeDtypeStruct((STEPS, blocks, LANES), jnp.float32),
        scratch_shapes=[pltpu.VMEM((blocks, 2 * STEPS * LANES), jnp.float32)],
        compiler_params=pltpu.CompilerParams(vmem_limit_bytes=48 << 20),
        name="coast_couple",
    )(got)


def local(
    adj_depth,
    conductance,
    wet,
    coast_cell,
    coast_dest,
    coast_node,
    coast_weight,
    adj_ocean,
    ocean_blocks,
    ocean_target,
):
    devices = lax.axis_size(("land", "sea"))
    group = lax.axis_size("sea")
    blocks = ocean_target.shape[0]
    width = adj_ocean.shape[1]
    land_out, masked = land_steps(adj_depth, conductance, wet)
    packs = packed(masked, coast_cell, coast_dest, coast_node, coast_weight, devices)
    packs = packs.reshape(STEPS + 1, devices, -1).transpose(1, 0, 2)
    got = lax.all_to_all(packs, ("land", "sea"), split_axis=0, concat_axis=0, tiled=True)
    coupled = coupled_steps(got.transpose(1, 0, 2).reshape(STEPS + 1, -1), blocks)

    target_flat = ocean_target.reshape(-1)
    marker = (
        target_flat[:, None] == jnp.arange(blocks * group, dtype=jnp.int32)[None, :]
    ).astype(jnp.float32)
    ocean_adj = adj_ocean
    for timestep in range(STEPS):
        ocean_low = ocean_adj.astype(jnp.bfloat16)
        terms = jnp.einsum(
            "bkij,bi->bkj", ocean_blocks, ocean_low, preferred_element_type=jnp.float32
        ).reshape(-1, width)
        summed = jnp.einsum("rc,rw->cw", marker, terms, precision=lax.Precision.HIGHEST)
        parts = lax.all_to_all(
            summed.reshape(group, blocks, width), "sea", split_axis=0, concat_axis=0, tiled=True
        )
        ocean_adj = 0.5 * ocean_adj + jnp.sum(parts, axis=0) + coupled[timestep]
    return (land_out, ocean_adj)


def solution(mesh):
    in_specs = (
        P("land", "sea"),
        P("land", "sea"),
        P(None, "land", "sea"),
        P(("land", "sea")),
        P(("land", "sea"), None),
        P(("land", "sea")),
        P(("land", "sea")),
        P(("land", "sea"), None),
        P(("land", "sea"), None, None, None),
        P(("land", "sea"), None),
    )
    out_specs = (P("land", "sea"), P(("land", "sea"), None))
    return jax.shard_map(local, mesh=mesh, in_specs=in_specs, out_specs=out_specs, check_vma=False)
```

```python
import functools

import jax
import jax.numpy as jnp
from jax import lax
from jax.experimental import pallas as pl
from jax.experimental.pallas import tpu as pltpu
from jax.sharding import PartitionSpec as P

STEPS = 4
LANES = 128
SUB = 8
HALO = STEPS


MESH = pl.DeviceIdType.MESH


def beside_of(axis):
    count, me = lax.axis_size(axis), lax.axis_index(axis)
    return lax.rem(me + count - 1, count), lax.rem(me + 1, count)


def land_kernel(depth, cond, wet, out, masked, ext, out_edge, in_edge, sends, recvs):
    rows, cols = depth.shape
    total = 2 + STEPS
    used = total * HALO
    height, width = ext.shape[1], ext.shape[2]
    mid_r, mid_c = pl.ds(SUB, rows), pl.ds(LANES, cols)
    west, east = beside_of("sea")
    north, south = beside_of("land")

    barrier = pltpu.get_barrier_semaphore()
    for to in ({"sea": west}, {"sea": east}, {"land": north}, {"land": south}):
        pl.semaphore_signal(barrier, inc=1, device_id=to, device_id_type=MESH)

    ext[0, mid_r, mid_c] = depth[...]
    ext[1, mid_r, mid_c] = cond[...]
    for t in range(STEPS):
        ext[2 + t, mid_r, mid_c] = wet[t].astype(jnp.float32)

    lane = lax.broadcasted_iota(jnp.int32, (rows, LANES), 1)

    def gathered(start, first):
        edge = jnp.zeros((rows, LANES), jnp.float32)
        for i in range(total):
            tile = ext[i, mid_r, pl.ds(start, LANES)]
            shift = (i * HALO - first) % LANES
            tile = pltpu.roll(tile, shift, 1) if shift else tile
            edge = jnp.where(lane // HALO == i, tile, edge)
        return edge.T[:used]

    out_edge[0] = gathered(LANES, 0)
    out_edge[1] = gathered(cols, LANES - HALO)
    for side in range(2):
        in_edge[side, used:, :] = jnp.zeros((LANES - used, rows), jnp.float32)
    pl.semaphore_wait(barrier, 4)

    copies = [
        pltpu.make_async_remote_copy(
            src_ref=out_edge.at[side],
            dst_ref=in_edge.at[side, pl.ds(0, used)],
            send_sem=sends.at[side],
            recv_sem=recvs.at[side],
            device_id={"sea": to},
            device_id_type=MESH,
        )
        for side, to in ((0, west), (1, east))
    ]
    for copy in copies:
        copy.start()
    for copy in copies:
        copy.wait()

    def spread_out(side, start, first, present):
        edge = in_edge[side].T
        for i in range(total):
            shift = (first - i * HALO) % LANES
            tile = pltpu.roll(edge, shift, 1) if shift else edge
            keep = (lane >= first) & (lane < first + HALO) & present
            ext[i, mid_r, pl.ds(start, LANES)] = jnp.where(keep, tile, 0.0)

    sea, seas = lax.axis_index("sea"), lax.axis_size("sea")
    land, lands = lax.axis_index("land"), lax.axis_size("land")
    spread_out(1, 0, LANES - HALO, sea > 0)
    spread_out(0, LANES + cols, 0, sea < seas - 1)

    copies = [
        pltpu.make_async_remote_copy(
            src_ref=ext.at[:, pl.ds(source, SUB), :],
            dst_ref=ext.at[:, pl.ds(target, SUB), :],
            send_sem=sends.at[slot],
            recv_sem=recvs.at[slot],
            device_id={"land": to},
            device_id_type=MESH,
        )
        for slot, source, target, to in (
            (2, SUB, SUB + rows, north),
            (3, rows, 0, south),
        )
    ]
    for copy in copies:
        copy.start()
    for copy in copies:
        copy.wait()
    for start, present in ((0, land > 0), (SUB + rows, land < lands - 1)):
        strip = ext[1, pl.ds(start, SUB), :]
        ext[1, pl.ds(start, SUB), :] = strip * jnp.where(present, 1.0, 0.0)

    for t in range(STEPS):
        wet_land = ext[2 + t] * ext[0]
        masked[t] = wet_land[SUB : SUB + rows, LANES : LANES + cols].astype(jnp.bfloat16)
        spread = ext[1] * wet_land
        beside = (
            pltpu.roll(spread, 1, 0)
            + pltpu.roll(spread, height - 1, 0)
            + pltpu.roll(spread, 1, 1)
            + pltpu.roll(spread, width - 1, 1)
        )
        ext[0] = ext[0] + (beside - 4.0 * spread)
    out[...] = ext[0, mid_r, mid_c]


def land_steps(depth, cond, wet):
    rows, cols = depth.shape
    total = 2 + STEPS
    vmem = pl.BlockSpec(memory_space=pltpu.VMEM)
    return pl.pallas_call(
        land_kernel,
        out_shape=(
            jax.ShapeDtypeStruct((rows, cols), jnp.float32),
            jax.ShapeDtypeStruct((STEPS, rows, cols), jnp.bfloat16),
        ),
        in_specs=[vmem] * 3,
        out_specs=(vmem, vmem),
        scratch_shapes=[
            pltpu.VMEM((total, rows + 2 * SUB, cols + 2 * LANES), jnp.float32),
            pltpu.VMEM((2, total * HALO, rows), jnp.float32),
            pltpu.VMEM((2, LANES, rows), jnp.float32),
            pltpu.SemaphoreType.DMA((4,)),
            pltpu.SemaphoreType.DMA((4,)),
        ],
        compiler_params=pltpu.CompilerParams(
            vmem_limit_bytes=40 << 20, collective_id=0, has_side_effects=True
        ),
        name="land_steps",
    )(depth, cond, wet)


def share_kernel(terms, target, ocean, coupled, out, summed, got, sends, recvs):
    group, me = lax.axis_size("sea"), lax.axis_index("sea")
    blocks = out.shape[0]
    others = [lax.rem(me + d, group) for d in range(1, group)]
    barrier = pltpu.get_barrier_semaphore()
    for to in others:
        pl.semaphore_signal(barrier, inc=1, device_id={"sea": to}, device_id_type=MESH)
    high, low = halves(terms[...])
    high, low = high.astype(jnp.bfloat16), low.astype(jnp.bfloat16)
    for s in range(group):
        at = iota((blocks, terms.shape[0]), 0) + s * blocks
        hot = jnp.where(at == target[...], 1.0, 0.0).astype(jnp.bfloat16)
        summed[s] = jnp.dot(hot, high, preferred_element_type=jnp.float32) + jnp.dot(
            hot, low, preferred_element_type=jnp.float32
        )
    pl.semaphore_wait(barrier, group - 1)
    copies = [
        pltpu.make_async_remote_copy(
            src_ref=summed.at[to],
            dst_ref=got.at[i],
            send_sem=sends.at[i],
            recv_sem=recvs.at[i],
            device_id={"sea": to},
            device_id_type=MESH,
        )
        for i, to in enumerate(others)
    ]
    for copy in copies:
        copy.start()
    result = 0.5 * ocean[...] + coupled[...] + summed[me]
    for copy in copies:
        copy.wait()
    for i in range(group - 1):
        result = result + got[i]
    out[...] = result


def shared_step(terms, target, ocean, coupled):
    group = lax.axis_size("sea")
    blocks, width = ocean.shape
    vmem = pl.BlockSpec(memory_space=pltpu.VMEM)
    return pl.pallas_call(
        share_kernel,
        out_shape=jax.ShapeDtypeStruct((blocks, width), jnp.float32),
        in_specs=[vmem] * 4,
        out_specs=vmem,
        scratch_shapes=[
            pltpu.VMEM((group, blocks, width), jnp.float32),
            pltpu.VMEM((group - 1, blocks, width), jnp.float32),
            pltpu.SemaphoreType.DMA((group - 1,)),
            pltpu.SemaphoreType.DMA((group - 1,)),
        ],
        compiler_params=pltpu.CompilerParams(collective_id=1, has_side_effects=True),
        name="ocean_share",
    )(terms, target, ocean, coupled)


def iota(shape, axis):
    return lax.broadcasted_iota(jnp.int32, shape, axis)


def halves(value):
    high = value.astype(jnp.bfloat16).astype(jnp.float32)
    return high, value - high


def across(a, b):
    return lax.dot_general(
        a, b, (((1,), (1,)), ((), ())), preferred_element_type=jnp.float32
    )


def placed(row, lane, values, rows):
    count = row.shape[1]
    row_hot = jnp.where(iota((rows, count), 0) == row, 1.0, 0.0).astype(jnp.bfloat16)
    lane_is = iota((LANES, count), 0) == lane
    spreads = [jnp.where(lane_is, v, 0.0).astype(jnp.bfloat16) for v in values]
    return across(row_hot, jnp.concatenate(spreads, axis=0))


def send_kernel(capacity, piece, cell, dest, node, weight, masked, out, acc, carry):
    step = pl.program_id(0)
    devices = carry.shape[0]
    cols = masked.shape[2]
    count = cell.shape[2]

    @pl.when(step == 0)
    def _():
        acc[...] = jnp.zeros_like(acc)
        carry[...] = jnp.zeros_like(carry)

    dest_now = dest[0]
    matches = jnp.where(iota((devices, count), 0) == dest_now, 1.0, 0.0)
    triangle = jnp.where(
        iota((piece, piece), 0) <= iota((piece, piece), 1), 1.0, 0.0
    ).astype(jnp.bfloat16)
    base = carry[:, 0:1]
    ranks = []
    for p in range(count // piece):
        own = matches[:, p * piece : (p + 1) * piece]
        running = jnp.dot(
            own.astype(jnp.bfloat16), triangle, preferred_element_type=jnp.float32
        )
        ranks.append(jnp.sum(own * (running + base), axis=0, keepdims=True))
        base = base + jnp.sum(own, axis=1, keepdims=True)
    carry[...] = jnp.broadcast_to(base, carry.shape)
    rank = jnp.concatenate(ranks, axis=1).astype(jnp.int32) - 1
    slot = dest_now * capacity + rank

    place = cell[0]
    cell_row, cell_col = place // cols, place % cols
    col_hot = jnp.where(iota((cols, count), 0) == cell_col, 1.0, 0.0).astype(jnp.bfloat16)
    row_is = iota((masked.shape[1], count), 0) == cell_row
    values = []
    for t in range(STEPS):
        lines = jnp.dot(masked[t], col_hot, preferred_element_type=jnp.float32)
        found = jnp.sum(jnp.where(row_is, lines, 0.0), axis=0, keepdims=True)
        values.extend(halves(weight[0] * found))
    node_now = node[0]
    values.append((node_now // LANES).astype(jnp.float32))
    values.append((node_now % LANES).astype(jnp.float32))
    acc[...] += placed(slot // LANES, slot % LANES, values, acc.shape[0])

    @pl.when(step == pl.num_programs(0) - 1)
    def _():
        def block(i):
            return acc[:, i * LANES : (i + 1) * LANES]

        for t in range(STEPS):
            out[t] = block(2 * t) + block(2 * t + 1)
        out[STEPS] = block(2 * STEPS) * float(LANES) + block(2 * STEPS + 1)


def packed(masked, cell, dest, node, weight, devices):
    entries = cell.shape[0]
    count = 1024
    steps = entries // count
    capacity = 2 * entries // devices
    rows = devices * capacity // LANES
    line = pl.BlockSpec((1, 1, count), lambda i: (i, 0, 0))
    shape = (steps, 1, count)
    return pl.pallas_call(
        functools.partial(send_kernel, capacity, 256),
        grid=(steps,),
        in_specs=[line] * 4 + [pl.BlockSpec(masked.shape, lambda i: (0, 0, 0))],
        out_specs=pl.BlockSpec((STEPS + 1, rows, LANES), lambda i: (0, 0, 0)),
        out_shape=jax.ShapeDtypeStruct((STEPS + 1, rows, LANES), jnp.float32),
        scratch_shapes=[
            pltpu.VMEM((rows, (2 * STEPS + 2) * LANES), jnp.float32),
            pltpu.VMEM((devices, LANES), jnp.float32),
        ],
        compiler_params=pltpu.CompilerParams(vmem_limit_bytes=48 << 20),
        name="coast_pack",
    )(cell.reshape(shape), dest.reshape(shape), node.reshape(shape), weight.reshape(shape), masked)


def couple_kernel(got, out, acc):
    step = pl.program_id(0)

    @pl.when(step == 0)
    def _():
        acc[...] = jnp.zeros_like(acc)

    node = got[STEPS : STEPS + 1, :].astype(jnp.int32)
    values = []
    for t in range(STEPS):
        values.extend(halves(got[t : t + 1, :]))
    acc[...] += placed(node // LANES, node % LANES, values, acc.shape[0])

    @pl.when(step == pl.num_programs(0) - 1)
    def _():
        for t in range(STEPS):
            at = 2 * t * LANES
            out[t] = acc[:, at : at + LANES] + acc[:, at + LANES : at + 2 * LANES]


def coupled_steps(got, blocks):
    slots = got.shape[1]
    count = 2048
    return pl.pallas_call(
        couple_kernel,
        grid=(slots // count,),
        in_specs=[pl.BlockSpec((STEPS + 1, count), lambda i: (0, i))],
        out_specs=pl.BlockSpec((STEPS, blocks, LANES), lambda i: (0, 0, 0)),
        out_shape=jax.ShapeDtypeStruct((STEPS, blocks, LANES), jnp.float32),
        scratch_shapes=[pltpu.VMEM((blocks, 2 * STEPS * LANES), jnp.float32)],
        compiler_params=pltpu.CompilerParams(vmem_limit_bytes=48 << 20),
        name="coast_couple",
    )(got)


def local(
    adj_depth,
    conductance,
    wet,
    coast_cell,
    coast_dest,
    coast_node,
    coast_weight,
    adj_ocean,
    ocean_blocks,
    ocean_target,
):
    devices = lax.axis_size(("land", "sea"))
    blocks = ocean_target.shape[0]
    width = adj_ocean.shape[1]
    land_out, masked = land_steps(adj_depth, conductance, wet)
    packs = packed(masked, coast_cell, coast_dest, coast_node, coast_weight, devices)
    packs = packs.reshape(STEPS + 1, devices, -1).transpose(1, 0, 2)
    got = lax.all_to_all(packs, ("land", "sea"), split_axis=0, concat_axis=0, tiled=True)
    coupled = coupled_steps(got.transpose(1, 0, 2).reshape(STEPS + 1, -1), blocks)

    target_row = ocean_target.reshape(1, -1)
    ocean_adj = adj_ocean
    for timestep in range(STEPS):
        ocean_low = ocean_adj.astype(jnp.bfloat16)
        terms = jnp.einsum(
            "bkij,bi->bkj", ocean_blocks, ocean_low, preferred_element_type=jnp.float32
        ).reshape(-1, width)
        ocean_adj = shared_step(terms, target_row, ocean_adj, coupled[timestep])
    return (land_out, ocean_adj)


def solution(mesh):
    in_specs = (
        P("land", "sea"),
        P("land", "sea"),
        P(None, "land", "sea"),
        P(("land", "sea")),
        P(("land", "sea"), None),
        P(("land", "sea")),
        P(("land", "sea")),
        P(("land", "sea"), None),
        P(("land", "sea"), None, None, None),
        P(("land", "sea"), None),
    )
    out_specs = (P("land", "sea"), P(("land", "sea"), None))
    return jax.shard_map(local, mesh=mesh, in_specs=in_specs, out_specs=out_specs, check_vma=False)
```
